32 devices in a mesh: groups: 2 (over y), frame: 4 (over z), query: 2 (over x), chan: 2 (over core).
Axes of the slice: x: 2, y: 2, z: 4, core: 2. Of those that a mesh axis runs over, the one named last changes fastest.
Arguments:
- features: bfloat16 [8, 64, 64, 256], P(('groups', 'frame'), None, None, 'chan'), parts along dimension 0, may hold values from -6 to 6
- query_frame: int32 [256], P(('groups', 'query')), parts along dimension 0, may hold values from 0 to 3
- query_pixel: int32 [256, 2], P(('groups', 'query')), parts along dimension 0, may hold values from 0 to 63
- conv_first: bfloat16 [3, 3, 1, 16], replicated, may hold values from -2 to 2
- conv_second: bfloat16 [3, 3, 16, 32], replicated, may hold values from -0.5 to 0.5
- depth_kernel: float32 [2, 3, 512], replicated, may hold values from -3 to 3
- w_in: bfloat16 [2, 2048, 512], P(None, ('frame', 'chan')), may hold values from -0.25 to 0.25
- w_out: bfloat16 [2, 2048, 512], P(None, ('frame', 'chan')), may hold values from -0.125 to 0.125
Outputs:
- tracks: bfloat16 [256, 4, 512], P(('groups', 'query'), 'frame'), parts along dimension 0
The draws below stay inside these ranges and needn't reach their ends.
There are 2 independent parts, one for each index of `groups`. The reference program is written for one: setup_inputs(seed, part) draws one part's arguments, and reference() takes and returns one part's arrays. A program takes and returns all parts, laid end to end along the dimension named above; an argument that names none is the same for every part. Nothing has to cross between parts.
All inputs are finite; a program needn't handle non-finite values.
Results may differ from the reference program's by a relative error of at most 0.02.
Values may be sent and summed in bfloat16 or wider, within the bound.
A program may use at most 64 MiB of HBM per device.

```python
import math
import jax
import jax.numpy as jnp
import numpy as np
from jax import lax

CHANNELS = 256
SIDE = 64
C1 = 16
C2 = 32
D = 512
HIDDEN_SIZE = 2048
MIXERS = 2
QRY_DEV = 64
FRAMES = 4
QUERIES = 128
N_QUERY = 2
N_CHAN = 2


def touch_ends(array, rng, smallest, largest):
    shape = array.shape
    spot = [jax.random.randint(jax.random.fold_in(rng, axis), (), 0, shape[axis]) for axis in range(len(shape))]
    array = array.at[tuple(spot)].set(smallest)
    longest = shape.index(max(shape))
    spot[longest] = (spot[longest] + 1) % shape[longest]
    return array.at[tuple(spot)].set(largest)


def block_levels(key, shape, split, smallest, largest):
    loudness = 1.0
    for dim, blocks in split:
        heights = jax.random.uniform(jax.random.fold_in(jax.random.fold_in(key, 6), dim), (blocks,), jnp.float32, smallest / len(split), largest / len(split))
        loudness = loudness * jnp.repeat(jnp.exp(heights), shape[dim] // blocks).reshape((-1,) + (1,) * (len(shape) - 1 - dim))
    return loudness


def rank_table(number_of, slope):
    loads = [(1 << 20) // math.isqrt(rank ** slope) + 1 for rank in range(1, number_of + 1)]
    width = 1 + sum(loads) // (1 << 30)
    return np.cumsum(np.array([max(1, weight // width) for weight in loads]))


def ranked_ids(own_key, dims, number_of, skew):
    table = rank_table(number_of, skew)
    lot = jax.random.randint(jax.random.fold_in(own_key, 1), dims, 0, int(table[number_of - 1]))
    rank = jnp.searchsorted(jnp.asarray(table, jnp.int32), lot, side="right")
    return jax.random.permutation(jax.random.fold_in(own_key, 2), number_of)[rank].astype(jnp.int32)


def scatter_about(stream_key, dims, deviation, limit, split=(), held_as=jnp.bfloat16):
    factor_of = block_levels(stream_key, dims, split, -0.22, 0.18) if split else 1.0
    values = jax.random.normal(stream_key, dims, jnp.float32) * deviation * factor_of
    return jnp.minimum(jnp.maximum(values, -limit), limit).astype(held_as)


def setup_inputs(seed: int = 0, part: int = 0) -> dict:
    seeds = jax.random.split(jax.random.key(seed), 9)
    part_keys = jax.random.split(jax.random.fold_in(seeds[8], part), 9)
    return {
        "features": scatter_about(part_keys[0], (FRAMES, SIDE, SIDE, CHANNELS), 1.0, 6.0, ((0, 4), (3, 2))),
        "query_frame": touch_ends(ranked_ids(part_keys[1], (QUERIES,), FRAMES, 2), jax.random.fold_in(part_keys[1], 3), 0, FRAMES - 1).astype(jnp.int32),
        "query_pixel": touch_ends(jax.random.randint(part_keys[2], (QUERIES, 2), 0, SIDE), jax.random.fold_in(part_keys[2], 1), 0, SIDE - 1).astype(jnp.int32),
        "conv_first": scatter_about(seeds[3], (3, 3, 1, C1), 9 ** -0.5, 2.0),
        "conv_second": scatter_about(seeds[4], (3, 3, C1, C2), (9 * C1) ** -0.5, 0.5),
        "depth_kernel": scatter_about(seeds[5], (MIXERS, 3, D), 0.6, 3.0, (), jnp.float32),
        "w_in": scatter_about(seeds[6], (MIXERS, HIDDEN_SIZE, D), D ** -0.5, 0.25, ((1, 8),)),
        "w_out": scatter_about(seeds[7], (MIXERS, HIDDEN_SIZE, D), HIDDEN_SIZE ** -0.5, 0.125, ((1, 8),)),
    }


def pool_maps(corr_maps, conv_first, conv_second):
    first_maps = lax.conv_general_dilated(corr_maps.astype(jnp.float32), conv_first.astype(jnp.float32), (2, 2), 'SAME', dimension_numbers=('HWCN', 'HWIO', 'HWCN'), preferred_element_type=jnp.float32)
    first_maps = jax.nn.relu(first_maps).astype(jnp.bfloat16)
    second_maps = lax.conv_general_dilated(first_maps.astype(jnp.float32), conv_second.astype(jnp.float32), (2, 2), 'SAME', dimension_numbers=('HWCN', 'HWIO', 'HWCN'), preferred_element_type=jnp.float32)
    second_maps = jax.nn.relu(second_maps)
    window = second_maps.shape[0] // 4
    pooled = second_maps.reshape(4, window, 4, window, second_maps.shape[2], second_maps.shape[3]).mean(axis=(1, 3))
    return pooled.reshape(16 * second_maps.shape[2], second_maps.shape[3]).T

def layer_norm(state):
    centre = state - lax.optimization_barrier(jnp.mean(state, axis=-1, keepdims=True))
    spread = lax.optimization_barrier(jnp.mean(centre * centre, axis=-1, keepdims=True))
    return (centre * lax.rsqrt(spread + 1e-05)).astype(jnp.bfloat16)

def depth_mix(padded, kernel):
    length = padded.shape[1] - 2
    wide = padded.astype(jnp.float32)
    summed = kernel[0] * wide[:, :length] + kernel[1] * wide[:, 1:length + 1] + kernel[2] * wide[:, 2:]
    return summed.astype(jnp.bfloat16)

def reference(features, query_frame, query_pixel, conv_first, conv_second, depth_kernel, w_in, w_out):
    query_vectors = features[query_frame, query_pixel[:, 0], query_pixel[:, 1], :]
    half_width = CHANNELS // N_CHAN
    corr_scale = 1.0 / math.sqrt(CHANNELS)

    def one_frame(frame_feat):
        flat = frame_feat.reshape(SIDE * SIDE, CHANNELS).astype(jnp.float32)
        summed = jnp.zeros((SIDE * SIDE, QUERIES), jnp.float32)
        for shard in range(N_CHAN):
            lower = shard * half_width
            local_corr = jnp.dot(flat[:, lower:lower + half_width], query_vectors[:, lower:lower + half_width].astype(jnp.float32).T)
            rounded = lax.optimization_barrier(local_corr.astype(jnp.bfloat16))
            summed = summed + rounded.astype(jnp.float32)
        corr_maps = (summed * corr_scale).astype(jnp.bfloat16).reshape(SIDE, SIDE, 1, QUERIES)
        return pool_maps(corr_maps, conv_first, conv_second)
    pooled = lax.map(one_frame, features)
    state = jnp.transpose(pooled, (1, 0, 2))
    for mixer in range(MIXERS):
        normed = layer_norm(state)
        padded = jnp.pad(normed, ((0, 0), (1, 1), (0, 0)))
        mixed = depth_mix(padded, depth_kernel[mixer])
        blocks = mixed.reshape(N_QUERY, QRY_DEV * FRAMES, D)
        weight_in = w_in[mixer].astype(jnp.float32)
        weight_out = w_out[mixer].astype(jnp.float32)

        def mlp_block(row_block):
            pre_act = jnp.dot(row_block.astype(jnp.float32), weight_in.T)
            hidden = jax.nn.gelu(pre_act, approximate=False).astype(jnp.bfloat16)
            return jnp.dot(hidden.astype(jnp.float32), weight_out)
        update = lax.map(mlp_block, blocks).reshape(QUERIES, FRAMES, D)
        state = state + update
    return state.astype(jnp.bfloat16)
```

```python
import functools
import math

import jax
import jax.numpy as jnp
from jax import lax
from jax.experimental import pallas as pl
from jax.experimental.pallas import tpu as pltpu
from jax.sharding import PartitionSpec as P

MESH = pl.DeviceIdType.MESH
F32 = jnp.float32
BF16 = jnp.bfloat16

ERF_TOP = (
    -2.72614225801306e-10,
    2.77068142495902e-08,
    -2.10102402082508e-06,
    -5.69250639462346e-05,
    -7.34990630326855e-04,
    -2.95459980854025e-03,
    -1.60960333262415e-02,
)
ERF_BOTTOM = (
    -1.45660718464996e-05,
    -2.13374055278905e-04,
    -1.68282697438203e-03,
    -7.37332916720468e-03,
    -1.42647390514189e-02,
)


def erf(x):
    x = jnp.clip(x, -4.0, 4.0)
    square = x * x
    top = jnp.full_like(x, ERF_TOP[0])
    for c in ERF_TOP[1:]:
        top = top * square + c
    bottom = jnp.full_like(x, ERF_BOTTOM[0])
    for c in ERF_BOTTOM[1:]:
        bottom = bottom * square + c
    return x * top / bottom


def gelu(x):
    return 0.5 * x * (1.0 + erf(x * math.sqrt(0.5)))


def layer_norm(state):
    centre = state - jnp.mean(state, axis=-1, keepdims=True)
    spread = jnp.mean(centre * centre, axis=-1, keepdims=True)
    return (centre * lax.rsqrt(spread + 1e-05)).astype(BF16)


def iota(shape, dim):
    return lax.broadcasted_iota(jnp.int32, shape, dim)


def log2(n):
    bits = n.bit_length() - 1
    assert 1 << bits == n
    return bits


def kernel(
    frames,
    side,
    corr_scale,
    feat_hbm,
    frame_ref,
    pixel_ref,
    conv1_ref,
    conv2_ref,
    depth_ref,
    win_hbm,
    wout_hbm,
    out_ref,
    feat,
    win,
    wout,
    qsend,
    qall,
    qsum,
    cbuf,
    crecv,
    cme,
    cmo,
    f1e,
    f1o,
    t1,
    t2,
    state,
    hall,
    pbuf,
    precv,
    psend,
    rrecv,
    outbuf,
    local_sem,
    q_send_sem,
    q_recv_sem,
    c_send_sem,
    c_recv_sem,
    g_send_sem,
    g_recv_sem,
    h_send_sem,
    h_recv_sem,
    p_send_sem,
    p_recv_sem,
    r_send_sem,
    r_recv_sem,
    o_send_sem,
    o_recv_sem,
):
    me = lax.axis_index("frame")
    core = lax.axis_index("chan")
    other = 1 - core
    peers = [lax.rem(me + d, frames) for d in range(frames)]
    sources = [lax.rem(me + frames - d, frames) for d in range(frames)]

    feat_copy = pltpu.make_async_copy(feat_hbm, feat, local_sem.at[0])
    feat_copy.start()
    win_copy = pltpu.make_async_copy(win_hbm, win, local_sem.at[1])
    win_copy.start()
    wout_copy = pltpu.make_async_copy(wout_hbm, wout, local_sem.at[2])
    wout_copy.start()

    barrier = pltpu.get_barrier_semaphore()
    for d in range(1, frames):
        pl.semaphore_signal(barrier, inc=1, device_id={"frame": peers[d]}, device_id_type=MESH)
    pl.semaphore_signal(barrier, inc=1, device_id={"chan": other}, device_id_type=MESH)

    queries = qsum.shape[0]
    half = queries // 2
    pixels = side * side
    mixers = win.shape[0]
    tile = 128
    blocks = pixels // tile
    pairs = blocks // 2

    local = jnp.where(
        frame_ref[...] == me, pixel_ref[0:1, :] * side + pixel_ref[1:2, :], -1
    ).astype(F32)
    diag = iota((queries, queries), 0) == iota((queries, queries), 1)
    column = jnp.sum(
        jnp.where(diag, jnp.broadcast_to(local, (queries, queries)), 0.0), axis=1, keepdims=True
    ).astype(jnp.int32)
    feat_copy.wait()
    step = 512
    picked = jnp.zeros((queries, feat.shape[1]), F32)
    lanes = iota((queries, step), 1)
    for k in range(pixels // step):
        hot = (lanes == (column - k * step)).astype(F32).astype(BF16)
        picked += jnp.dot(hot, feat[k * step : (k + 1) * step, :], preferred_element_type=F32)
    qsend[...] = picked.astype(BF16)

    pl.semaphore_wait(barrier, frames)
    q_copies = []
    for d in range(frames - 1, 0, -1):
        copy = pltpu.make_async_remote_copy(
            src_ref=qsend,
            dst_ref=qall.at[d - 1],
            send_sem=q_send_sem.at[d - 1],
            recv_sem=q_recv_sem.at[d - 1],
            device_id={"frame": peers[d]},
            device_id_type=MESH,
        )
        copy.start()
        q_copies.append(copy)

    c1 = conv1_ref.shape[1]
    c2 = conv2_ref.shape[1]
    wide = (side // 2) * c1
    spread1 = (iota((c1, wide), 0) == (iota((c1, wide), 1) & (c1 - 1))).astype(F32).astype(BF16)
    rows1 = jnp.dot(conv1_ref[...], spread1, preferred_element_type=F32)
    offset = iota((side, wide), 0) - 2 * (iota((side, wide), 1) >> log2(c1))
    for a in range(3):
        band = jnp.zeros((side, wide), F32)
        for b in range(3):
            band = jnp.where(offset == b, rows1[3 * a + b : 3 * a + b + 1, :], band)
        t1[a * side : (a + 1) * side, :] = band.astype(BF16)
    t1[3 * side :, :] = jnp.zeros((t1.shape[0] - 3 * side, wide), BF16)
    spread2 = (iota((c2, tile), 0) == (iota((c2, tile), 1) & (c2 - 1))).astype(F32).astype(BF16)
    rows2 = jnp.dot(conv2_ref[...], spread2, preferred_element_type=F32)
    cells = 2 * tile // c1
    offset = iota((cells, c1, tile), 0) - 2 * (iota((cells, c1, tile), 2) >> log2(c2))
    for a in range(3):
        band = jnp.zeros((cells, c1, tile), F32)
        for b in range(3):
            start = (3 * a + b) * c1
            band = jnp.where(offset == b, rows2[start : start + c1, :][None], band)
        t2[a] = band.reshape(cells * c1, tile).astype(BF16)
    cme[pairs] = jnp.zeros((half, tile), BF16)
    f1e[pairs] = jnp.zeros((half, f1e.shape[2]), BF16)
    f1e[:, :, wide:] = jnp.zeros((f1e.shape[0], half, tile), BF16)
    f1o[:, :, wide:] = jnp.zeros((f1o.shape[0], half, tile), BF16)

    total = qsend[...].astype(F32)
    for copy in q_copies:
        copy.wait()
    for d in range(1, frames):
        total += qall[d - 1].astype(F32)
    vectors = total.astype(BF16)

    chunks = c_send_sem.shape[0]
    per = blocks // chunks
    c_copies = []
    for k in range(chunks):
        corr = lax.dot_general(
            vectors,
            feat[k * per * tile : (k + 1) * per * tile, :],
            (((1,), (1,)), ((), ())),
            preferred_element_type=F32,
        ).astype(BF16)
        for h in range(2):
            for i in range(per):
                cbuf[h, k * per + i] = corr[h * half : (h + 1) * half, i * tile : (i + 1) * tile]
        copy = pltpu.make_async_remote_copy(
            src_ref=cbuf.at[other, pl.ds(k * per, per)],
            dst_ref=crecv.at[pl.ds(k * per, per)],
            send_sem=c_send_sem.at[k],
            recv_sem=c_recv_sem.at[k],
            device_id={"chan": other},
            device_id_type=MESH,
        )
        copy.start()
        c_copies.append(copy)
    for k in range(chunks):
        c_copies[k].wait()
        for i in range(k * per, (k + 1) * per):
            summed = cbuf[core, i].astype(F32) + crecv[i].astype(F32)
            value = (summed * corr_scale).astype(BF16)
            if i % 2 == 0:
                cme[i // 2] = value
            else:
                cmo[i // 2] = value

    window = pairs // 4
    for r in range(0, pairs, window):
        rows = window * half
        even = cme[r : r + window].reshape(rows, tile)
        odd = cmo[r : r + window].reshape(rows, tile)
        after = cme[r + 1 : r + window + 1].reshape(rows, tile)
        for first, second, dest in ((even, odd, f1e), (odd, after, f1o)):
            maps = jnp.dot(
                jnp.concatenate([first, second], axis=1), t1[...], preferred_element_type=F32
            )
            dest[r : r + window, :, :wide] = (
                jnp.maximum(maps, 0.0).astype(BF16).reshape(window, half, wide)
            )
    group = iota((half, tile), 1) >> log2(c2)
    cols = wide // tile
    for r in range(0, pairs, window):
        rows = window * half
        packed = jnp.zeros((half, tile), F32)
        for u in range(cols):
            span = slice(u * tile, (u + 2) * tile)
            maps = jnp.dot(
                f1e[r : r + window, :, span].reshape(rows, 2 * tile),
                t2[0],
                preferred_element_type=F32,
            )
            maps += jnp.dot(
                f1o[r : r + window, :, span].reshape(rows, 2 * tile),
                t2[1],
                preferred_element_type=F32,
            )
            maps += jnp.dot(
                f1e[r + 1 : r + window + 1, :, span].reshape(rows, 2 * tile),
                t2[2],
                preferred_element_type=F32,
            )
            pooled = jnp.sum(jnp.maximum(maps, 0.0).reshape(window, half, tile), axis=0)
            pooled = pooled + pltpu.roll(pooled, tile // 2, 1)
            pooled = pooled + pltpu.roll(pooled, c2, 1)
            packed = jnp.where(group == u, pooled, packed)
        part = r // window
        state[:, part * tile : (part + 1) * tile] = packed * (1.0 / (window * window))

    pending = []
    for m in range(mixers):
        normed = layer_norm(state[...])
        hall[m, me, core] = normed
        mine = hall.at[m, me, core]
        g_copies = {}
        for d in range(frames - 1, 0, -1):
            copy = pltpu.make_async_remote_copy(
                src_ref=mine,
                dst_ref=mine,
                send_sem=g_send_sem.at[m, d - 1],
                recv_sem=g_recv_sem.at[m, d - 1],
                device_id={"frame": peers[d]},
                device_id_type=MESH,
            )
            copy.start()
            g_copies[d] = copy
        h_copies = []
        for d in range(frames):
            if d:
                g_copies[d].wait_recv()
            block = hall.at[m, sources[d], core]
            copy = pltpu.make_async_remote_copy(
                src_ref=block,
                dst_ref=block,
                send_sem=h_send_sem.at[m, d],
                recv_sem=h_recv_sem.at[m, d],
                device_id={"chan": other},
                device_id_type=MESH,
            )
            copy.start()
            h_copies.append(copy)
        for copy in h_copies:
            copy.wait()
        for copy in g_copies.values():
            copy.wait_send()
        if m == 0:
            win_copy.wait()
            wout_copy.wait()
        width = hall.shape[4]
        taps = [depth_ref[m, j : j + 1, :] for j in range(3)]
        blocks_of = [hall[m, f].reshape(queries, width).astype(F32) for f in range(frames)]
        zero = jnp.zeros((queries, width), F32)
        p_copies = []
        for f in range(frames):
            before = blocks_of[f - 1] if f else zero
            behind = blocks_of[f + 1] if f + 1 < frames else zero
            mixed = (taps[0] * before + taps[1] * blocks_of[f] + taps[2] * behind).astype(BF16)
            pre = lax.dot_general(
                mixed, win[m], (((1,), (1,)), ((), ())), preferred_element_type=F32
            )
            hidden = gelu(pre).astype(BF16)
            update = jnp.dot(hidden, wout[m], preferred_element_type=F32).astype(BF16)
            pbuf[m, f] = update.reshape(2, half, width)
            copy = pltpu.make_async_remote_copy(
                src_ref=pbuf.at[m, f, other],
                dst_ref=precv.at[m, f],
                send_sem=p_send_sem.at[m, f],
                recv_sem=p_recv_sem.at[m, f],
                device_id={"chan": other},
                device_id_type=MESH,
            )
            copy.start()
            p_copies.append(copy)
        for copy in p_copies:
            copy.wait()
        r_copies = []
        for d in range(frames - 1, 0, -1):
            psend[m, d] = (
                pbuf[m, peers[d], core].astype(F32) + precv[m, peers[d]].astype(F32)
            ).astype(BF16)
            copy = pltpu.make_async_remote_copy(
                src_ref=psend.at[m, d],
                dst_ref=rrecv.at[m, d - 1],
                send_sem=r_send_sem.at[m, d - 1],
                recv_sem=r_recv_sem.at[m, d - 1],
                device_id={"frame": peers[d]},
                device_id_type=MESH,
            )
            copy.start()
            r_copies.append(copy)
        total = pbuf[m, me, core].astype(F32) + precv[m, me].astype(F32)
        for copy in r_copies:
            copy.wait()
        for d in range(1, frames):
            total += rrecv[m, d - 1].astype(F32)
        state[...] = state[...] + total

    outbuf[core] = state[...].astype(BF16)
    copy = pltpu.make_async_remote_copy(
        src_ref=outbuf.at[core],
        dst_ref=outbuf.at[core],
        send_sem=o_send_sem,
        recv_sem=o_recv_sem,
        device_id={"chan": other},
        device_id_type=MESH,
    )
    copy.start()
    copy.wait()
    out_ref[...] = outbuf[...].reshape(queries, outbuf.shape[2])


def on_device(
    features, query_frame, query_pixel, conv_first, conv_second, depth_kernel, w_in, w_out
):
    frames = lax.axis_size("frame")
    chans = lax.axis_size("chan")
    local_frames, side, _, chan_width = features.shape
    queries = query_frame.shape[0]
    mixers, hidden, width = w_in.shape
    c1 = conv_first.shape[3]
    c2 = conv_second.shape[3]
    half = queries // 2
    pixels = side * side
    blocks = pixels // 128
    wide = side // 2 * c1
    assert local_frames == 1 and chans == 2 and side == 64 and wide == width == 16 * c2
    any_space = pl.BlockSpec(memory_space=pl.ANY)
    vmem = pl.BlockSpec(memory_space=pltpu.VMEM)
    dma = pltpu.SemaphoreType.DMA
    chunks = 4
    out = pl.pallas_call(
        functools.partial(kernel, frames, side, 1.0 / math.sqrt(chan_width * chans)),
        out_shape=jax.ShapeDtypeStruct((queries, width), BF16),
        in_specs=[any_space, vmem, vmem, vmem, vmem, vmem, any_space, any_space],
        out_specs=vmem,
        scratch_shapes=[
            pltpu.VMEM((pixels, chan_width), BF16),
            pltpu.VMEM((mixers, hidden, width), BF16),
            pltpu.VMEM((mixers, hidden, width), BF16),
            pltpu.VMEM((queries, chan_width), BF16),
            pltpu.VMEM((frames - 1, queries, chan_width), BF16),
            pltpu.VMEM((queries, chan_width), BF16),
            pltpu.VMEM((2, blocks, half, 128), BF16),
            pltpu.VMEM((blocks, half, 128), BF16),
            pltpu.VMEM((blocks // 2 + 1, half, 128), BF16),
            pltpu.VMEM((blocks // 2, half, 128), BF16),
            pltpu.VMEM((blocks // 2 + 1, half, wide + 128), BF16),
            pltpu.VMEM((blocks // 2, half, wide + 128), BF16),
            pltpu.VMEM((4 * side, wide), BF16),
            pltpu.VMEM((3, 256, 128), BF16),
            pltpu.VMEM((half, width), F32),
            pltpu.VMEM((mixers, frames, 2, half, width), BF16),
            pltpu.VMEM((mixers, frames, 2, half, width), BF16),
            pltpu.VMEM((mixers, frames, half, width), BF16),
            pltpu.VMEM((mixers, frames, half, width), BF16),
            pltpu.VMEM((mixers, frames - 1, half, width), BF16),
            pltpu.VMEM((2, half, width), BF16),
            dma((3,)),
            dma((frames - 1,)),
            dma((frames - 1,)),
            dma((chunks,)),
            dma((chunks,)),
            dma((mixers, frames - 1)),
            dma((mixers, frames - 1)),
            dma((mixers, frames)),
            dma((mixers, frames)),
            dma((mixers, frames)),
            dma((mixers, frames)),
            dma((mixers, frames - 1)),
            dma((mixers, frames - 1)),
            dma,
            dma,
        ],
        compiler_params=pltpu.CompilerParams(
            collective_id=0, has_side_effects=True, vmem_limit_bytes=48 * 1024 * 1024
        ),
        name="track_step",
    )(
        features.reshape(pixels, chan_width),
        query_frame.reshape(1, queries),
        query_pixel.T,
        conv_first.reshape(9, c1),
        conv_second.reshape(9 * c1, c2),
        depth_kernel,
        w_in,
        w_out,
    )
    return out.reshape(queries, 1, width)


def solution(mesh):
    in_specs = (
        P(("groups", "frame"), None, None, "chan"),
        P(("groups", "query")),
        P(("groups", "query"), None),
        P(),
        P(),
        P(),
        P(None, ("frame", "chan"), None),
        P(None, ("frame", "chan"), None),
    )
    out_specs = P(("groups", "query"), "frame", None)
    return jax.shard_map(
        on_device, mesh=mesh, in_specs=in_specs, out_specs=out_specs, check_vma=False
    )
```

```python
import functools
import math

import jax
import jax.numpy as jnp
from jax import lax
from jax.experimental import pallas as pl
from jax.experimental.pallas import tpu as pltpu
from jax.sharding import PartitionSpec as P

MESH = pl.DeviceIdType.MESH
F32 = jnp.float32
BF16 = jnp.bfloat16

ERF_TOP = (
    -2.72614225801306e-10,
    2.77068142495902e-08,
    -2.10102402082508e-06,
    -5.69250639462346e-05,
    -7.34990630326855e-04,
    -2.95459980854025e-03,
    -1.60960333262415e-02,
)
ERF_BOTTOM = (
    -1.45660718464996e-05,
    -2.13374055278905e-04,
    -1.68282697438203e-03,
    -7.37332916720468e-03,
    -1.42647390514189e-02,
)


def erf(x):
    x = jnp.clip(x, -4.0, 4.0)
    square = x * x
    top = jnp.full_like(x, ERF_TOP[0])
    for c in ERF_TOP[1:]:
        top = top * square + c
    bottom = jnp.full_like(x, ERF_BOTTOM[0])
    for c in ERF_BOTTOM[1:]:
        bottom = bottom * square + c
    return x * top / bottom


def gelu(x):
    return 0.5 * x * (1.0 + erf(x * math.sqrt(0.5)))


def layer_norm(state):
    centre = state - jnp.mean(state, axis=-1, keepdims=True)
    spread = jnp.mean(centre * centre, axis=-1, keepdims=True)
    return (centre * lax.rsqrt(spread + 1e-05)).astype(BF16)


def iota(shape, dim):
    return lax.broadcasted_iota(jnp.int32, shape, dim)


def log2(n):
    bits = n.bit_length() - 1
    assert 1 << bits == n
    return bits


def kernel(
    frames,
    side,
    corr_scale,
    feat_hbm,
    frame_ref,
    pixel_ref,
    conv1_ref,
    conv2_ref,
    depth_ref,
    win_hbm,
    wout_hbm,
    out_ref,
    feat,
    win,
    wout,
    qsend,
    qall,
    qsum,
    cbuf,
    crecv,
    cme,
    cmo,
    f1e,
    f1o,
    t1,
    t2,
    state,
    hall,
    pbuf,
    rrecv,
    outbuf,
    local_sem,
    q_send_sem,
    q_recv_sem,
    c_send_sem,
    c_recv_sem,
    g_send_sem,
    g_recv_sem,
    w_send_sem,
    w_recv_sem,
    r_send_sem,
    r_recv_sem,
    o_send_sem,
    o_recv_sem,
):
    me = lax.axis_index("frame")
    core = lax.axis_index("chan")
    other = 1 - core
    peers = [lax.rem(me + d, frames) for d in range(frames)]
    sources = [lax.rem(me + frames - d, frames) for d in range(frames)]

    feat_copy = pltpu.make_async_copy(feat_hbm, feat, local_sem.at[0])
    feat_copy.start()
    w_copies = [
        pltpu.make_async_copy(win_hbm, win.at[core], local_sem.at[1]),
        pltpu.make_async_copy(wout_hbm, wout.at[core], local_sem.at[2]),
    ]
    for copy in w_copies:
        copy.start()

    barrier = pltpu.get_barrier_semaphore()
    for d in range(1, frames):
        pl.semaphore_signal(barrier, inc=1, device_id={"frame": peers[d]}, device_id_type=MESH)
    pl.semaphore_signal(barrier, inc=1, device_id={"chan": other}, device_id_type=MESH)

    queries = qsum.shape[0]
    half = queries // 2
    pixels = side * side
    mixers = win.shape[1]
    tile = 128
    blocks = pixels // tile
    pairs = blocks // 2

    local = jnp.where(
        frame_ref[...] == me, pixel_ref[0:1, :] * side + pixel_ref[1:2, :], -1
    ).astype(F32)
    diag = iota((queries, queries), 0) == iota((queries, queries), 1)
    column = jnp.sum(
        jnp.where(diag, jnp.broadcast_to(local, (queries, queries)), 0.0), axis=1, keepdims=True
    ).astype(jnp.int32)
    feat_copy.wait()
    step = 512
    picked = jnp.zeros((queries, feat.shape[1]), F32)
    lanes = iota((queries, step), 1)
    for k in range(pixels // step):
        hot = (lanes == (column - k * step)).astype(F32).astype(BF16)
        picked += jnp.dot(hot, feat[k * step : (k + 1) * step, :], preferred_element_type=F32)
    qsend[...] = picked.astype(BF16)

    pl.semaphore_wait(barrier, frames)
    q_copies = []
    for d in range(frames - 1, 0, -1):
        copy = pltpu.make_async_remote_copy(
            src_ref=qsend,
            dst_ref=qall.at[d - 1],
            send_sem=q_send_sem.at[d - 1],
            recv_sem=q_recv_sem.at[d - 1],
            device_id={"frame": peers[d]},
            device_id_type=MESH,
        )
        copy.start()
        q_copies.append(copy)

    for j, (source, dest) in enumerate(((win_hbm, win), (wout_hbm, wout))):
        copy = pltpu.make_async_remote_copy(
            src_ref=source,
            dst_ref=dest.at[core],
            send_sem=w_send_sem.at[j],
            recv_sem=w_recv_sem.at[j],
            device_id={"chan": other},
            device_id_type=MESH,
        )
        copy.start()
        w_copies.append(copy)

    c1 = conv1_ref.shape[2]
    c2 = conv2_ref.shape[1]
    wide = (side // 2) * c1
    spread1 = (iota((c1, wide), 0) == (iota((c1, wide), 1) & (c1 - 1))).astype(F32).astype(BF16)
    offset = iota((side, wide), 0) - 2 * (iota((side, wide), 1) >> log2(c1))
    for a in range(3):
        rows1 = jnp.dot(conv1_ref[a], spread1, preferred_element_type=F32)
        band = jnp.zeros((side, wide), F32)
        for b in range(3):
            band = jnp.where(offset == b, rows1[b : b + 1, :], band)
        t1[a * side : (a + 1) * side, :] = band.astype(BF16)
    t1[3 * side :, :] = jnp.zeros((t1.shape[0] - 3 * side, wide), BF16)
    spread2 = (iota((c2, tile), 0) == (iota((c2, tile), 1) & (c2 - 1))).astype(F32).astype(BF16)
    rows2 = jnp.dot(conv2_ref[...], spread2, preferred_element_type=F32)
    cells = 2 * tile // c1
    offset = iota((cells, c1, tile), 0) - 2 * (iota((cells, c1, tile), 2) >> log2(c2))
    for a in range(3):
        band = jnp.zeros((cells, c1, tile), F32)
        for b in range(3):
            start = (3 * a + b) * c1
            band = jnp.where(offset == b, rows2[start : start + c1, :][None], band)
        t2[a] = band.reshape(cells * c1, tile).astype(BF16)
    cme[pairs] = jnp.zeros((half, tile), BF16)
    f1e[pairs] = jnp.zeros((half, f1e.shape[2]), BF16)
    f1e[:, :, wide:] = jnp.zeros((f1e.shape[0], half, tile), BF16)
    f1o[:, :, wide:] = jnp.zeros((f1o.shape[0], half, tile), BF16)

    total = qsend[...].astype(F32)
    for copy in q_copies:
        copy.wait()
    for d in range(1, frames):
        total += qall[d - 1].astype(F32)
    vectors = total.astype(BF16)

    chunks = c_send_sem.shape[0]
    per = blocks // chunks
    c_copies = []
    for k in range(chunks):
        corr = lax.dot_general(
            vectors,
            feat[k * per * tile : (k + 1) * per * tile, :],
            (((1,), (1,)), ((), ())),
            preferred_element_type=F32,
        ).astype(BF16)
        for h in range(2):
            for i in range(per):
                cbuf[h, k * per + i] = corr[h * half : (h + 1) * half, i * tile : (i + 1) * tile]
        copy = pltpu.make_async_remote_copy(
            src_ref=cbuf.at[other, pl.ds(k * per, per)],
            dst_ref=crecv.at[pl.ds(k * per, per)],
            send_sem=c_send_sem.at[k],
            recv_sem=c_recv_sem.at[k],
            device_id={"chan": other},
            device_id_type=MESH,
        )
        copy.start()
        c_copies.append(copy)
    for k in range(chunks):
        c_copies[k].wait()
        for i in range(k * per, (k + 1) * per):
            summed = cbuf[core, i].astype(F32) + crecv[i].astype(F32)
            value = (summed * corr_scale).astype(BF16)
            if i % 2 == 0:
                cme[i // 2] = value
            else:
                cmo[i // 2] = value

    window = pairs // 4
    for r in range(0, pairs, window):
        rows = window * half
        even = cme[r : r + window].reshape(rows, tile)
        odd = cmo[r : r + window].reshape(rows, tile)
        after = cme[r + 1 : r + window + 1].reshape(rows, tile)
        for first, second, dest in ((even, odd, f1e), (odd, after, f1o)):
            maps = jnp.dot(
                jnp.concatenate([first, second], axis=1), t1[...], preferred_element_type=F32
            )
            dest[r : r + window, :, :wide] = (
                jnp.maximum(maps, 0.0).astype(BF16).reshape(window, half, wide)
            )
    group = iota((half, tile), 1) >> log2(c2)
    cols = wide // tile
    for r in range(0, pairs, window):
        rows = window * half
        packed = jnp.zeros((half, tile), F32)
        for u in range(cols):
            span = slice(u * tile, (u + 2) * tile)
            maps = jnp.dot(
                f1e[r : r + window, :, span].reshape(rows, 2 * tile),
                t2[0],
                preferred_element_type=F32,
            )
            maps += jnp.dot(
                f1o[r : r + window, :, span].reshape(rows, 2 * tile),
                t2[1],
                preferred_element_type=F32,
            )
            maps += jnp.dot(
                f1e[r + 1 : r + window + 1, :, span].reshape(rows, 2 * tile),
                t2[2],
                preferred_element_type=F32,
            )
            pooled = jnp.sum(jnp.maximum(maps, 0.0).reshape(window, half, tile), axis=0)
            pooled = pooled + pltpu.roll(pooled, tile // 2, 1)
            pooled = pooled + pltpu.roll(pooled, c2, 1)
            packed = jnp.where(group == u, pooled, packed)
        part = r // window
        state[:, part * tile : (part + 1) * tile] = packed * (1.0 / (window * window))

    for m in range(mixers):
        normed = layer_norm(state[...])
        hall[m, me] = normed
        mine = hall.at[m, me]
        g_copies = {}
        for d in range(frames - 1, 0, -1):
            copy = pltpu.make_async_remote_copy(
                src_ref=mine,
                dst_ref=mine,
                send_sem=g_send_sem.at[m, d - 1],
                recv_sem=g_recv_sem.at[m, d - 1],
                device_id={"frame": peers[d]},
                device_id_type=MESH,
            )
            copy.start()
            g_copies[d] = copy
        for copy in g_copies.values():
            copy.wait()
        if m == 0:
            for copy in w_copies:
                copy.wait()
        width = hall.shape[3]
        taps = [depth_ref[j, m : m + 1, :] for j in range(3)]
        blocks_of = [hall[m, f].astype(F32) for f in range(frames)]
        zero = jnp.zeros((half, width), F32)
        mixed = []
        for f in range(frames):
            before = blocks_of[f - 1] if f else zero
            behind = blocks_of[f + 1] if f + 1 < frames else zero
            mixed.append(
                (taps[0] * before + taps[1] * blocks_of[f] + taps[2] * behind).astype(BF16)
            )
        mixed = jnp.concatenate(mixed, axis=0)
        update = jnp.zeros((frames * half, width), F32)
        for c in range(2):
            pre = lax.dot_general(
                mixed, win[c, m], (((1,), (1,)), ((), ())), preferred_element_type=F32
            )
            hidden = gelu(pre).astype(BF16)
            update += jnp.dot(hidden, wout[c, m], preferred_element_type=F32)
        pbuf[m] = update.astype(BF16).reshape(frames, half, width)
        r_copies = []
        for d in range(frames - 1, 0, -1):
            copy = pltpu.make_async_remote_copy(
                src_ref=pbuf.at[m, peers[d]],
                dst_ref=rrecv.at[m, d - 1],
                send_sem=r_send_sem.at[m, d - 1],
                recv_sem=r_recv_sem.at[m, d - 1],
                device_id={"frame": peers[d]},
                device_id_type=MESH,
            )
            copy.start()
            r_copies.append(copy)
        total = state[...] + pbuf[m, me].astype(F32)
        for copy in r_copies:
            copy.wait()
        for d in range(1, frames):
            total += rrecv[m, d - 1].astype(F32)
        state[...] = total

    outbuf[core] = state[...].astype(BF16)
    copy = pltpu.make_async_remote_copy(
        src_ref=outbuf.at[core],
        dst_ref=outbuf.at[core],
        send_sem=o_send_sem,
        recv_sem=o_recv_sem,
        device_id={"chan": other},
        device_id_type=MESH,
    )
    copy.start()
    copy.wait()
    out_ref[...] = outbuf[...].reshape(queries, outbuf.shape[2])


def on_device(
    features, query_frame, query_pixel, conv_first, conv_second, depth_kernel, w_in, w_out
):
    frames = lax.axis_size("frame")
    chans = lax.axis_size("chan")
    local_frames, side, _, chan_width = features.shape
    queries = query_frame.shape[0]
    mixers, hidden, width = w_in.shape
    c1 = conv_first.shape[3]
    c2 = conv_second.shape[3]
    half = queries // 2
    pixels = side * side
    blocks = pixels // 128
    wide = side // 2 * c1
    assert local_frames == 1 and chans == 2 and side == 64 and wide == width == 16 * c2
    any_space = pl.BlockSpec(memory_space=pl.ANY)
    vmem = pl.BlockSpec(memory_space=pltpu.VMEM)
    dma = pltpu.SemaphoreType.DMA
    chunks = 4
    out = pl.pallas_call(
        functools.partial(kernel, frames, side, 1.0 / math.sqrt(chan_width * chans)),
        out_shape=jax.ShapeDtypeStruct((queries, width), BF16),
        in_specs=[any_space, vmem, vmem, vmem, vmem, vmem, any_space, any_space],
        out_specs=vmem,
        scratch_shapes=[
            pltpu.VMEM((pixels, chan_width), BF16),
            pltpu.VMEM((2, mixers, hidden, width), BF16),
            pltpu.VMEM((2, mixers, hidden, width), BF16),
            pltpu.VMEM((queries, chan_width), BF16),
            pltpu.VMEM((frames - 1, queries, chan_width), BF16),
            pltpu.VMEM((queries, chan_width), BF16),
            pltpu.VMEM((2, blocks, half, 128), BF16),
            pltpu.VMEM((blocks, half, 128), BF16),
            pltpu.VMEM((blocks // 2 + 1, half, 128), BF16),
            pltpu.VMEM((blocks // 2, half, 128), BF16),
            pltpu.VMEM((blocks // 2 + 1, half, wide + 128), BF16),
            pltpu.VMEM((blocks // 2, half, wide + 128), BF16),
            pltpu.VMEM((4 * side, wide), BF16),
            pltpu.VMEM((3, 256, 128), BF16),
            pltpu.VMEM((half, width), F32),
            pltpu.VMEM((mixers, frames, half, width), BF16),
            pltpu.VMEM((mixers, frames, half, width), BF16),
            pltpu.VMEM((mixers, frames - 1, half, width), BF16),
            pltpu.VMEM((2, half, width), BF16),
            dma((3,)),
            dma((frames - 1,)),
            dma((frames - 1,)),
            dma((chunks,)),
            dma((chunks,)),
            dma((mixers, frames - 1)),
            dma((mixers, frames - 1)),
            dma((2,)),
            dma((2,)),
            dma((mixers, frames - 1)),
            dma((mixers, frames - 1)),
            dma,
            dma,
        ],
        compiler_params=pltpu.CompilerParams(
            collective_id=0, has_side_effects=True
        ),
        name="track_step",
    )(
        features.reshape(pixels, chan_width),
        query_frame.reshape(1, queries),
        query_pixel.T,
        conv_first.transpose(0, 2, 1, 3).reshape(3, 3, c1),
        conv_second.reshape(9 * c1, c2),
        depth_kernel.transpose(1, 0, 2),
        w_in,
        w_out,
    )
    return out.reshape(queries, 1, width)


def solution(mesh):
    in_specs = (
        P(("groups", "frame"), None, None, "chan"),
        P(("groups", "query")),
        P(("groups", "query"), None),
        P(),
        P(),
        P(),
        P(None, ("frame", "chan"), None),
        P(None, ("frame", "chan"), None),
    )
    out_specs = P(("groups", "query"), "frame", None)
    return jax.shard_map(
        on_device, mesh=mesh, in_specs=in_specs, out_specs=out_specs, check_vma=False
    )
```

```python
import functools
import math

import jax
import jax.numpy as jnp
from jax import lax
from jax.experimental import pallas as pl
from jax.experimental.pallas import tpu as pltpu
from jax.sharding import PartitionSpec as P

MESH = pl.DeviceIdType.MESH
F32 = jnp.float32
BF16 = jnp.bfloat16

ERF_TOP = (
    -2.72614225801306e-10,
    2.77068142495902e-08,
    -2.10102402082508e-06,
    -5.69250639462346e-05,
    -7.34990630326855e-04,
    -2.95459980854025e-03,
    -1.60960333262415e-02,
)
ERF_BOTTOM = (
    -1.45660718464996e-05,
    -2.13374055278905e-04,
    -1.68282697438203e-03,
    -7.37332916720468e-03,
    -1.42647390514189e-02,
)


def erf(x):
    x = jnp.clip(x, -4.0, 4.0)
    square = x * x
    top = jnp.full_like(x, ERF_TOP[0])
    for c in ERF_TOP[1:]:
        top = top * square + c
    bottom = jnp.full_like(x, ERF_BOTTOM[0])
    for c in ERF_BOTTOM[1:]:
        bottom = bottom * square + c
    return x * top / bottom


def gelu(x):
    return 0.5 * x * (1.0 + erf(x * math.sqrt(0.5)))


def layer_norm(state):
    centre = state - jnp.mean(state, axis=-1, keepdims=True)
    spread = jnp.mean(centre * centre, axis=-1, keepdims=True)
    return (centre * lax.rsqrt(spread + 1e-05)).astype(BF16)


def iota(shape, dim):
    return lax.broadcasted_iota(jnp.int32, shape, dim)


def log2(n):
    bits = n.bit_length() - 1
    assert 1 << bits == n
    return bits


def kernel(
    frames,
    side,
    corr_scale,
    feat_hbm,
    frame_ref,
    pixel_ref,
    conv1_ref,
    conv2_ref,
    depth_ref,
    win_hbm,
    wout_hbm,
    out_ref,
    feat,
    win,
    wout,
    qsend,
    qall,
    qsum,
    cbuf,
    crecv,
    cme,
    cmo,
    f1e,
    f1o,
    t1,
    t2,
    state,
    hall,
    pbuf,
    rrecv,
    outbuf,
    local_sem,
    q_send_sem,
    q_recv_sem,
    c_send_sem,
    c_recv_sem,
    g_send_sem,
    g_recv_sem,
    w_send_sem,
    w_recv_sem,
    r_send_sem,
    r_recv_sem,
    o_send_sem,
    o_recv_sem,
):
    me = lax.axis_index("frame")
    core = lax.axis_index("chan")
    other = 1 - core
    peers = [lax.rem(me + d, frames) for d in range(frames)]

    feat_copy = pltpu.make_async_copy(feat_hbm, feat, local_sem.at[0])
    feat_copy.start()
    w_copies = [
        pltpu.make_async_copy(win_hbm, win.at[core], local_sem.at[1]),
        pltpu.make_async_copy(wout_hbm, wout.at[core], local_sem.at[2]),
    ]
    for copy in w_copies:
        copy.start()

    barrier = pltpu.get_barrier_semaphore()
    for d in range(1, frames):
        pl.semaphore_signal(barrier, inc=1, device_id={"frame": peers[d]}, device_id_type=MESH)
    pl.semaphore_signal(barrier, inc=1, device_id={"chan": other}, device_id_type=MESH)

    queries = qsum.shape[0]
    half = queries // 2
    pixels = side * side
    mixers = win.shape[1]
    tile = 128
    blocks = pixels // tile
    pairs = blocks // 2

    local = jnp.where(
        frame_ref[...] == me, pixel_ref[0:1, :] * side + pixel_ref[1:2, :], -1
    ).astype(F32)
    diag = iota((queries, queries), 0) == iota((queries, queries), 1)
    column = jnp.sum(
        jnp.where(diag, jnp.broadcast_to(local, (queries, queries)), 0.0), axis=1, keepdims=True
    ).astype(jnp.int32)
    feat_copy.wait()
    step = 512
    picked = jnp.zeros((queries, feat.shape[1]), F32)
    lanes = iota((queries, step), 1)
    for k in range(pixels // step):
        hot = (lanes == (column - k * step)).astype(F32).astype(BF16)
        picked += jnp.dot(hot, feat[k * step : (k + 1) * step, :], preferred_element_type=F32)
    qsend[...] = picked.astype(BF16)

    pl.semaphore_wait(barrier, frames)
    q_copies = []
    for d in range(frames - 1, 0, -1):
        copy = pltpu.make_async_remote_copy(
            src_ref=qsend,
            dst_ref=qall.at[d - 1],
            send_sem=q_send_sem.at[d - 1],
            recv_sem=q_recv_sem.at[d - 1],
            device_id={"frame": peers[d]},
            device_id_type=MESH,
        )
        copy.start()
        q_copies.append(copy)

    for j, (source, dest) in enumerate(((win_hbm, win), (wout_hbm, wout))):
        copy = pltpu.make_async_remote_copy(
            src_ref=source,
            dst_ref=dest.at[core],
            send_sem=w_send_sem.at[j],
            recv_sem=w_recv_sem.at[j],
            device_id={"chan": other},
            device_id_type=MESH,
        )
        copy.start()
        w_copies.append(copy)

    c1 = conv1_ref.shape[2]
    c2 = conv2_ref.shape[1]
    wide = (side // 2) * c1
    spread1 = (iota((c1, wide), 0) == (iota((c1, wide), 1) & (c1 - 1))).astype(F32).astype(BF16)
    offset = iota((side, wide), 0) - 2 * (iota((side, wide), 1) >> log2(c1))
    for a in range(3):
        rows1 = jnp.dot(conv1_ref[a], spread1, preferred_element_type=F32)
        band = jnp.zeros((side, wide), F32)
        for b in range(3):
            band = jnp.where(offset == b, rows1[b : b + 1, :], band)
        t1[a * side : (a + 1) * side, :] = band.astype(BF16)
    t1[3 * side :, :] = jnp.zeros((t1.shape[0] - 3 * side, wide), BF16)
    spread2 = (iota((c2, tile), 0) == (iota((c2, tile), 1) & (c2 - 1))).astype(F32).astype(BF16)
    rows2 = jnp.dot(conv2_ref[...], spread2, preferred_element_type=F32)
    cells = 2 * tile // c1
    offset = iota((cells, c1, tile), 0) - 2 * (iota((cells, c1, tile), 2) >> log2(c2))
    for a in range(3):
        band = jnp.zeros((cells, c1, tile), F32)
        for b in range(3):
            start = (3 * a + b) * c1
            band = jnp.where(offset == b, rows2[start : start + c1, :][None], band)
        t2[a] = band.reshape(cells * c1, tile).astype(BF16)
    cme[pairs] = jnp.zeros((half, tile), BF16)
    for m in range(mixers):
        hall[m, 0] = jnp.zeros(state.shape, BF16)
        hall[m, frames + 1] = jnp.zeros(state.shape, BF16)
    f1e[pairs] = jnp.zeros((half, f1e.shape[2]), BF16)
    f1e[:, :, wide:] = jnp.zeros((f1e.shape[0], half, tile), BF16)
    f1o[:, :, wide:] = jnp.zeros((f1o.shape[0], half, tile), BF16)

    total = qsend[...].astype(F32)
    for copy in q_copies:
        copy.wait()
    for d in range(1, frames):
        total += qall[d - 1].astype(F32)
    vectors = total.astype(BF16)

    chunks = c_send_sem.shape[0]
    per = blocks // chunks
    c_copies = []
    for k in range(chunks):
        corr = lax.dot_general(
            vectors,
            feat[k * per * tile : (k + 1) * per * tile, :],
            (((1,), (1,)), ((), ())),
            preferred_element_type=F32,
        ).astype(BF16)
        for h in range(2):
            for i in range(per):
                cbuf[h, k * per + i] = corr[h * half : (h + 1) * half, i * tile : (i + 1) * tile]
        copy = pltpu.make_async_remote_copy(
            src_ref=cbuf.at[other, pl.ds(k * per, per)],
            dst_ref=crecv.at[pl.ds(k * per, per)],
            send_sem=c_send_sem.at[k],
            recv_sem=c_recv_sem.at[k],
            device_id={"chan": other},
            device_id_type=MESH,
        )
        copy.start()
        c_copies.append(copy)
    for k in range(chunks):
        c_copies[k].wait()
        for i in range(k * per, (k + 1) * per):
            summed = cbuf[core, i].astype(F32) + crecv[i].astype(F32)
            value = (summed * corr_scale).astype(BF16)
            if i % 2 == 0:
                cme[i // 2] = value
            else:
                cmo[i // 2] = value

    window = pairs // 4
    for r in range(0, pairs, window):
        rows = window * half
        even = cme[r : r + window].reshape(rows, tile)
        odd = cmo[r : r + window].reshape(rows, tile)
        after = cme[r + 1 : r + window + 1].reshape(rows, tile)
        for first, second, dest in ((even, odd, f1e), (odd, after, f1o)):
            maps = jnp.dot(
                jnp.concatenate([first, second], axis=1), t1[...], preferred_element_type=F32
            )
            dest[r : r + window, :, :wide] = (
                jnp.maximum(maps, 0.0).astype(BF16).reshape(window, half, wide)
            )
    group = iota((half, tile), 1) >> log2(c2)
    cols = wide // tile
    for r in range(0, pairs, window):
        rows = window * half
        packed = jnp.zeros((half, tile), F32)
        for u in range(cols):
            span = slice(u * tile, (u + 2) * tile)
            maps = jnp.dot(
                f1e[r : r + window, :, span].reshape(rows, 2 * tile),
                t2[0],
                preferred_element_type=F32,
            )
            maps += jnp.dot(
                f1o[r : r + window, :, span].reshape(rows, 2 * tile),
                t2[1],
                preferred_element_type=F32,
            )
            maps += jnp.dot(
                f1e[r + 1 : r + window + 1, :, span].reshape(rows, 2 * tile),
                t2[2],
                preferred_element_type=F32,
            )
            pooled = jnp.sum(jnp.maximum(maps, 0.0).reshape(window, half, tile), axis=0)
            pooled = pooled + pltpu.roll(pooled, tile // 2, 1)
            pooled = pooled + pltpu.roll(pooled, c2, 1)
            packed = jnp.where(group == u, pooled, packed)
        part = r // window
        state[:, part * tile : (part + 1) * tile] = packed * (1.0 / (window * window))

    for m in range(mixers):
        normed = layer_norm(state[...])
        hall[m, me + 1] = normed
        mine = hall.at[m, me + 1]
        g_copies = {}
        for d in range(frames - 1, 0, -1):
            copy = pltpu.make_async_remote_copy(
                src_ref=mine,
                dst_ref=mine,
                send_sem=g_send_sem.at[m, d - 1],
                recv_sem=g_recv_sem.at[m, d - 1],
                device_id={"frame": peers[d]},
                device_id_type=MESH,
            )
            copy.start()
            g_copies[d] = copy
        for copy in g_copies.values():
            copy.wait()
        if m == 0:
            for copy in w_copies:
                copy.wait()
        width = hall.shape[3]
        taps = [depth_ref[j, m : m + 1, :] for j in range(3)]
        r_copies = []
        for k in range(frames):
            f = jnp.where(2 * me < frames, frames - 1 - k, k)
            mixed = (
                taps[0] * hall[m, f].astype(F32)
                + taps[1] * hall[m, f + 1].astype(F32)
                + taps[2] * hall[m, f + 2].astype(F32)
            ).astype(BF16)
            update = jnp.zeros((half, width), F32)
            for c in range(2):
                pre = lax.dot_general(
                    mixed, win[c, m], (((1,), (1,)), ((), ())), preferred_element_type=F32
                )
                hidden = gelu(pre).astype(BF16)
                update += jnp.dot(hidden, wout[c, m], preferred_element_type=F32)
            pbuf[m, k] = update.astype(BF16)
            copy = pltpu.make_async_remote_copy(
                src_ref=pbuf.at[m, k],
                dst_ref=rrecv.at[m, me],
                send_sem=r_send_sem.at[m, k],
                recv_sem=r_recv_sem.at[m, me],
                device_id={"frame": f},
                device_id_type=MESH,
            )
            r_copies.append((f, copy))

            @pl.when(f != me)
            def _():
                copy.start()

            @pl.when(f == me)
            def _():
                rrecv[m, me] = pbuf[m, k]

        for f, copy in r_copies:

            @pl.when(f != me)
            def _():
                copy.wait_send()

        for source in range(frames):

            @pl.when(source != me)
            def _():
                pltpu.make_async_remote_copy(
                    src_ref=pbuf.at[m, source],
                    dst_ref=rrecv.at[m, source],
                    send_sem=r_send_sem.at[m, source],
                    recv_sem=r_recv_sem.at[m, source],
                    device_id={"frame": source},
                    device_id_type=MESH,
                ).wait_recv()

        total = state[...]
        for source in range(frames):
            total += rrecv[m, source].astype(F32)
        state[...] = total

    outbuf[core] = state[...].astype(BF16)
    copy = pltpu.make_async_remote_copy(
        src_ref=outbuf.at[core],
        dst_ref=outbuf.at[core],
        send_sem=o_send_sem,
        recv_sem=o_recv_sem,
        device_id={"chan": other},
        device_id_type=MESH,
    )
    copy.start()
    copy.wait()
    out_ref[...] = outbuf[...].reshape(queries, outbuf.shape[2])


def on_device(
    features, query_frame, query_pixel, conv_first, conv_second, depth_kernel, w_in, w_out
):
    frames = lax.axis_size("frame")
    chans = lax.axis_size("chan")
    local_frames, side, _, chan_width = features.shape
    queries = query_frame.shape[0]
    mixers, hidden, width = w_in.shape
    c1 = conv_first.shape[3]
    c2 = conv_second.shape[3]
    half = queries // 2
    pixels = side * side
    blocks = pixels // 128
    wide = side // 2 * c1
    assert local_frames == 1 and chans == 2 and side == 64 and wide == width == 16 * c2
    any_space = pl.BlockSpec(memory_space=pl.ANY)
    vmem = pl.BlockSpec(memory_space=pltpu.VMEM)
    dma = pltpu.SemaphoreType.DMA
    chunks = 4
    out = pl.pallas_call(
        functools.partial(kernel, frames, side, 1.0 / math.sqrt(chan_width * chans)),
        out_shape=jax.ShapeDtypeStruct((queries, width), BF16),
        in_specs=[any_space, vmem, vmem, vmem, vmem, vmem, any_space, any_space],
        out_specs=vmem,
        scratch_shapes=[
            pltpu.VMEM((pixels, chan_width), BF16),
            pltpu.VMEM((2, mixers, hidden, width), BF16),
            pltpu.VMEM((2, mixers, hidden, width), BF16),
            pltpu.VMEM((queries, chan_width), BF16),
            pltpu.VMEM((frames - 1, queries, chan_width), BF16),
            pltpu.VMEM((queries, chan_width), BF16),
            pltpu.VMEM((2, blocks, half, 128), BF16),
            pltpu.VMEM((blocks, half, 128), BF16),
            pltpu.VMEM((blocks // 2 + 1, half, 128), BF16),
            pltpu.VMEM((blocks // 2, half, 128), BF16),
            pltpu.VMEM((blocks // 2 + 1, half, wide + 128), BF16),
            pltpu.VMEM((blocks // 2, half, wide + 128), BF16),
            pltpu.VMEM((4 * side, wide), BF16),
            pltpu.VMEM((3, 256, 128), BF16),
            pltpu.VMEM((half, width), F32),
            pltpu.VMEM((mixers, frames + 2, half, width), BF16),
            pltpu.VMEM((mixers, frames, half, width), BF16),
            pltpu.VMEM((mixers, frames, half, width), BF16),
            pltpu.VMEM((2, half, width), BF16),
            dma((3,)),
            dma((frames - 1,)),
            dma((frames - 1,)),
            dma((chunks,)),
            dma((chunks,)),
            dma((mixers, frames - 1)),
            dma((mixers, frames - 1)),
            dma((2,)),
            dma((2,)),
            dma((mixers, frames)),
            dma((mixers, frames)),
            dma,
            dma,
        ],
        compiler_params=pltpu.CompilerParams(
            collective_id=0, has_side_effects=True
        ),
        name="track_step",
    )(
        features.reshape(pixels, chan_width),
        query_frame.reshape(1, queries),
        query_pixel.T,
        conv_first.transpose(0, 2, 1, 3).reshape(3, 3, c1),
        conv_second.reshape(9 * c1, c2),
        depth_kernel.transpose(1, 0, 2),
        w_in,
        w_out,
    )
    return out.reshape(queries, 1, width)


def solution(mesh):
    in_specs = (
        P(("groups", "frame"), None, None, "chan"),
        P(("groups", "query")),
        P(("groups", "query"), None),
        P(),
        P(),
        P(),
        P(None, ("frame", "chan"), None),
        P(None, ("frame", "chan"), None),
    )
    out_specs = P(("groups", "query"), "frame", None)
    return jax.shard_map(
        on_device, mesh=mesh, in_specs=in_specs, out_specs=out_specs, check_vma=False
    )
```
